256 devices in a mesh: blk: 64 (over x, z, y_lo), uly: 4 (over y_hi, core).
Axes of the slice: x: 4, y: 4 (y_hi: 2, y_lo: 2; y = y_hi * 2 + y_lo), z: 8, core: 2. Of those that a mesh axis runs over, the one named last changes fastest.
Arguments:
- tokens: bfloat16 [6144, 2560], P(('blk', 'uly')), may hold values from -6 to 6
- in_bits: int32 [6144, 2560], P(('blk', 'uly')), may hold values from 0 to 1
- qkv_weights: bfloat16 [2, 3, 2560, 2560], P(None, None, 'blk', 'uly'), may hold values from -0.125 to 0.125
- qkv_bits: int32 [6144, 3, 2560], P('blk', None, 'uly'), may hold values from 0 to 1
- gain_query: float32 [2560], P('uly'), may hold values from 0.7 to 1.8
- gain_key: float32 [2560], P('uly'), may hold values from 0.7 to 1.8
- out_weights: bfloat16 [2, 2560, 2560], P(None, 'uly', 'blk'), may hold values from -0.5 to 0.5
- mix_bits: int32 [6144, 2560], P('blk', 'uly'), may hold values from 0 to 1
- out_bits: int32 [6144, 2560], P('blk'), may hold values from 0 to 1
Outputs:
- layer_output: bfloat16 [6144, 2560], P(('blk', 'uly'))
The draws below stay inside these ranges and needn't reach their ends.
Inputs may be any that keep to these rules, and one draw needn't show every extreme that they name: `in_bits`: a bit of 1 stands for the sign +1, a bit of 0 for -1. `qkv_bits`: a bit of 1 stands for the sign +1, a bit of 0 for -1. `mix_bits`: a bit of 1 stands for the sign +1, a bit of 0 for -1. `out_bits`: a bit of 1 stands for the sign +1, a bit of 0 for -1.
All inputs are finite; a program needn't handle non-finite values.
Results may differ from the reference program's by a relative error of at most 0.018.
Values may be sent and summed in bfloat16 or wider, within the bound.
A program may use at most 128 MiB of HBM per device.

```python
import math
import jax
import jax.numpy as jnp
from jax import lax

D = 2560
HEADS = 20
HEAD = 128
TOKENS = 6144


def touch_ends(drawn, rng, smallest, top_value):
    longest = drawn.shape.index(max(drawn.shape))
    spots = []
    for shift in (0, 1):
        where = [jax.random.randint(jax.random.fold_in(rng, axis), (), 0, length) for axis, length in enumerate(drawn.shape)]
        where[longest] = (where[longest] + shift) % drawn.shape[longest]
        spots.append(tuple(where))
    return drawn.at[spots[0]].set(smallest).at[spots[1]].set(top_value)


def block_levels(own_key, extent, shards, smallest, largest):
    gain, own = 1.0, jax.random.fold_in(own_key, 6)
    for position, blocks in shards:
        heights = jnp.exp(jax.random.uniform(jax.random.fold_in(own, position), (blocks,), jnp.float32, smallest / len(shards), largest / len(shards)))
        gain = gain * jnp.repeat(heights, extent[position] // blocks).reshape([-1 if axis == position else 1 for axis in range(len(extent))])
    return gain


def normal_values(key, extent, deviation, most, pieces=(), held_as=jnp.bfloat16):
    level = block_levels(key, extent, pieces, -0.22, 0.18) if pieces else 1.0
    values = jax.random.normal(key, extent, jnp.float32) * deviation * level
    return jnp.minimum(jnp.maximum(values, -most), most).astype(held_as)


def setup_inputs(seed: int = 0) -> dict:
    keys = jax.random.split(jax.random.key(seed), 10)
    return {
        "tokens": normal_values(keys[0], (TOKENS, D), 1.0, 6.0, ((0, 256),)),
        "in_bits": touch_ends(jax.random.randint(keys[1], (TOKENS, D), 0, 2), jax.random.fold_in(keys[1], 1), 0, 1).astype(jnp.int32),
        "qkv_weights": normal_values(keys[2], (2, 3, D, HEADS * HEAD), D ** -0.5, 0.125, ((2, 64), (3, 4))),
        "qkv_bits": touch_ends(jax.random.randint(keys[3], (TOKENS, 3, HEADS * HEAD), 0, 2), jax.random.fold_in(keys[3], 1), 0, 1).astype(jnp.int32),
        "gain_query": jnp.clip(jnp.exp(math.log(1.8) - 0.9444616 * jax.random.uniform(keys[4], (HEADS * HEAD,), jnp.float32) ** block_levels(keys[4], (HEADS * HEAD,), ((0, 4),), -0.2, 0.2)), 0.7, 1.8),
        "gain_key": jnp.clip(jnp.exp(math.log(1.8) - 0.9444616 * jax.random.uniform(keys[5], (HEADS * HEAD,), jnp.float32) ** block_levels(keys[5], (HEADS * HEAD,), ((0, 4),), -0.2, 0.2)), 0.7, 1.8),
        "out_weights": normal_values(keys[6], (2, HEADS * HEAD, D), (HEADS * HEAD // 16) ** -0.5, 0.5, ((1, 4), (2, 64))),
        "mix_bits": touch_ends(jax.random.randint(keys[7], (TOKENS, HEADS * HEAD), 0, 2), jax.random.fold_in(keys[7], 1), 0, 1).astype(jnp.int32),
        "out_bits": touch_ends(jax.random.randint(keys[8], (TOKENS, D), 0, 2), jax.random.fold_in(keys[8], 1), 0, 1).astype(jnp.int32),
    }


epsilon = 1e-06

def signed(bit_values):
    return (2 * bit_values - 1).astype(jnp.float32)

def normalize(values, gain_vector):
    row_count = values.shape[0]
    by_head = values.astype(jnp.float32).reshape(row_count, -1, HEAD)
    inverse_rms = lax.rsqrt(lax.optimization_barrier(jnp.mean(by_head * by_head, axis=-1, keepdims=True)) + epsilon)
    return (by_head * inverse_rms * gain_vector.reshape(-1, HEAD)).astype(jnp.bfloat16)

def reference(tokens, in_bits, qkv_weights, qkv_bits, gain_query, gain_key, out_weights, mix_bits, out_bits):
    flipped = (tokens.astype(jnp.float32) * signed(in_bits)).astype(jnp.bfloat16)
    qkv_signs = signed(qkv_bits)
    projections = []
    for qkv_slot in range(3):
        mean_part = jnp.dot(tokens, qkv_weights[0, qkv_slot], preferred_element_type=jnp.float32)
        delta_part = jnp.dot(flipped, qkv_weights[1, qkv_slot], preferred_element_type=jnp.float32)
        projections.append((mean_part + qkv_signs[:, qkv_slot] * delta_part).astype(jnp.bfloat16))
    queries = normalize(projections[0], gain_query)
    keys_normed = normalize(projections[1], gain_key)
    values_all = projections[2].reshape(projections[2].shape[0], -1, HEAD)
    score_scale = 1.0 / math.sqrt(HEAD)

    def one_head(operands):
        query_head, key_head, value_head = operands
        scores = jnp.dot(query_head, key_head.T, preferred_element_type=jnp.float32) * score_scale
        weights = jnp.exp(scores).astype(jnp.bfloat16)
        totals = lax.optimization_barrier(jnp.sum(weights.astype(jnp.float32), axis=1))
        return (jnp.dot(weights, value_head, preferred_element_type=jnp.float32) / totals[:, None]).astype(jnp.bfloat16)
    heads_out = lax.map(one_head, (jnp.transpose(queries, (1, 0, 2)), jnp.transpose(keys_normed, (1, 0, 2)), jnp.transpose(values_all, (1, 0, 2))))
    attended = jnp.transpose(heads_out, (1, 0, 2)).reshape(tokens.shape[0], -1)
    attended_flipped = (attended.astype(jnp.float32) * signed(mix_bits)).astype(jnp.bfloat16)
    mean_out = jnp.dot(attended, out_weights[0], preferred_element_type=jnp.float32)
    delta_out = jnp.dot(attended_flipped, out_weights[1], preferred_element_type=jnp.float32)
    return (mean_out + signed(out_bits) * delta_out).astype(jnp.bfloat16)
```

```python
import functools
import math

import jax
import jax.numpy as jnp
from jax import lax
from jax.experimental import pallas as pl
from jax.experimental.pallas import tpu as pltpu
from jax.sharding import PartitionSpec as P

HEAD = 128
NX, NY, NZ, NC = 4, 4, 8, 2
GROUP = 8
EPSILON = 1e-06
MESH = pl.DeviceIdType.MESH
BF16 = jnp.bfloat16
F32 = jnp.float32


def signed(bits):
    return (2 * bits - 1).astype(F32)


def place():
    blk, uly = lax.axis_index("blk"), lax.axis_index("uly")
    return blk // 16, (uly // 2) * 2 + blk % 2, (blk // 2) % 8, uly % 2


def device(x, y, z, c):
    return {"blk": x * 16 + z * 2 + y % 2, "uly": (y // 2) * 2 + c}


def row_slot(x, y, c):
    return x * 8 + (y % 2) * 4 + (y // 2) * 2 + c


class Mover:
    def __init__(self, send, recv, me):
        self.send, self.recv, self.me, self.sent = send, recv, me, []

    def put(self, src, dst, slot, where):
        copy = pltpu.make_async_remote_copy(
            src_ref=src,
            dst_ref=dst,
            send_sem=self.send.at[len(self.sent)],
            recv_sem=self.recv.at[slot],
            device_id=where,
            device_id_type=MESH,
        )
        copy.start()
        self.sent.append(copy)

    def got(self, ref, slot):
        pltpu.make_async_remote_copy(
            src_ref=ref,
            dst_ref=ref,
            send_sem=self.send.at[0],
            recv_sem=self.recv.at[slot],
            device_id=self.me,
            device_id_type=MESH,
        ).wait_recv()

    def finish(self):
        for copy in self.sent:
            copy.wait_send()


def greet(partners):
    barrier = pltpu.get_barrier_semaphore()
    for partner in partners:
        pl.semaphore_signal(barrier, inc=1, device_id=partner, device_id_type=MESH)
    pl.semaphore_wait(barrier, len(partners))


def group_peer(x, y, z, c, d):
    there = (x * 2 + y % 2 + d) % GROUP
    return device(there // 2, (y // 2) * 2 + there % 2, z, c), there


def comm(kernel, args, outs, sends, recvs, locals_, collective_id):
    return pl.pallas_call(
        kernel,
        out_shape=outs,
        in_specs=[pl.BlockSpec(memory_space=pl.ANY)] * len(args),
        out_specs=[pl.BlockSpec(memory_space=pl.ANY)] * len(outs),
        scratch_shapes=[
            pltpu.SemaphoreType.DMA((sends,)),
            pltpu.SemaphoreType.DMA((recvs,)),
            pltpu.SemaphoreType.DMA((locals_,)),
        ],
        compiler_params=pltpu.CompilerParams(collective_id=collective_id, has_side_effects=True),
    )(*args)


def gather_kernel(xs, wj, wo, sg, xg, wg, wog, sgg, send, recv, loc):
    x, y, z, c = place()
    low = y % 2
    me = device(x, y, z, c)
    own_group = x * 2 + low
    a = x * (1 - c) + y * c
    b = y * (1 - c) + x * c

    def at(first, second):
        return first * (1 - c) + second * c, second * (1 - c) + first * c

    def dev_at(first, second):
        px, py = at(first % 4, second % 4)
        return device(px, py, z, c)

    def slot_at(first, second):
        px, py = at(first % 4, second % 4)
        return row_slot(px, py, c)

    a_up, a_down = dev_at(a + 1, b), dev_at(a + 3, b)
    b_up, b_down = dev_at(a, b + 1), dev_at(a, b + 3)
    z_up, z_down = device(x, y, (z + 1) % NZ, c), device(x, y, (z + 7) % NZ, c)
    twin = device(x, y, z, 1 - c)
    peers = [group_peer(x, y, z, c, d) for d in range(1, GROUP)]
    other_y = device(x, (y + 3 + 2 * (y % 2)) % 4, z, c)
    greet([peer for peer, _ in peers] + [other_y, twin, z_up, z_down])

    mover = Mover(send, recv, me)
    own = slot_at(a, b)
    local = [
        pltpu.make_async_copy(wj.at[own_group], wg.at[:, x, z, low], loc.at[0]),
        pltpu.make_async_copy(xs, xg.at[:, own], loc.at[1]),
        pltpu.make_async_copy(wo, wog.at[:, z], loc.at[2]),
        pltpu.make_async_copy(sg.at[own_group], sgg.at[own_group], loc.at[3]),
    ]
    for copy in local:
        copy.start()

    def w_slot(d):
        return d - 1

    def s_slot(d):
        return 7 + d - 1

    A1, A2, B1U, B1D, B2U, B2D, TWIN, ZW, ZO = 14, 16, 18, 22, 26, 30, 34, 50, 58

    for d, (peer, there) in enumerate(peers, 1):
        mover.put(wj.at[there], wg.at[:, x, z, low], w_slot(d), peer)
    mover.put(xs, xg.at[:, own], A1, a_up)
    mover.put(xs, xg.at[:, own], A1 + 1, a_down)
    mover.put(xs, xg.at[:, own], B1U, b_up)
    mover.put(xs, xg.at[:, own], B1D, b_down)
    mover.put(xs, xg.at[:, own], TWIN, twin)
    for d, (peer, there) in enumerate(peers, 1):
        mover.put(sg.at[there], sgg.at[own_group], s_slot(d), peer)

    local[0].wait()
    for d in range(1, GROUP):
        mover.got(wg.at[:, x, z, low], w_slot(d))

    def z_step(t, source_down, source_up):
        if t < 4:
            mover.put(wg.at[:, :, source_down], wg.at[:, :, source_down], ZW + 2 * (t - 1), z_up)
            mover.put(wg.at[:, :, source_up], wg.at[:, :, source_up], ZW + 2 * (t - 1) + 1, z_down)
        else:
            mover.put(wg.at[0, :, source_down], wg.at[0, :, source_down], ZW + 6, z_up)
            mover.put(wg.at[1, :, source_up], wg.at[1, :, source_up], ZW + 7, z_down)

    def o_step(t, source_down, source_up):
        if t < 4:
            mover.put(wog.at[:, source_down], wog.at[:, source_down], ZO + 2 * (t - 1), z_up)
            mover.put(wog.at[:, source_up], wog.at[:, source_up], ZO + 2 * (t - 1) + 1, z_down)
        else:
            mover.put(wog.at[0, source_down], wog.at[0, source_down], ZO + 6, z_up)
            mover.put(wog.at[1, source_up], wog.at[1, source_up], ZO + 7, z_down)

    def z_got(t):
        down, up = (z + 8 - t) % NZ, (z + t) % NZ
        mover.got(wg.at[:, :, down], ZW + 2 * (t - 1))
        mover.got(wg.at[:, :, up], ZW + 2 * (t - 1) + 1)
        return down, up

    def o_got(t):
        down, up = (z + 8 - t) % NZ, (z + t) % NZ
        mover.got(wog.at[:, down], ZO + 2 * (t - 1))
        mover.got(wog.at[:, up], ZO + 2 * (t - 1) + 1)
        return down, up

    z_step(1, z, z)

    def spread(slot, k):
        shard = xg.at[:, slot]
        mover.put(shard, shard, B1U + k, b_up)
        mover.put(shard, shard, B1D + k, b_down)
        mover.put(shard, shard, TWIN + k, twin)

    from_down, from_up, far = slot_at(a + 3, b), slot_at(a + 1, b), slot_at(a + 2, b)
    mover.got(xg.at[:, from_down], A1)
    mover.put(xg.at[0, from_down], xg.at[0, from_down], A2, a_up)
    spread(from_down, 1)
    mover.got(xg.at[:, from_up], A1 + 1)
    mover.put(xg.at[1, from_up], xg.at[1, from_up], A2 + 1, a_down)
    spread(from_up, 2)
    local[2].wait()
    mover.got(xg.at[0, far], A2)
    mover.got(xg.at[1, far], A2 + 1)
    spread(far, 3)

    def second(k, first):
        down, up = slot_at(first, b + 3), slot_at(first, b + 1)
        mover.got(xg.at[:, down], B1U + k)
        mover.put(xg.at[0, down], xg.at[0, down], B2U + k, b_up)
        mover.put(xg.at[:, down], xg.at[:, down], TWIN + 4 + k, twin)
        mover.got(xg.at[:, up], B1D + k)
        mover.put(xg.at[1, up], xg.at[1, up], B2D + k, b_down)
        mover.put(xg.at[:, up], xg.at[:, up], TWIN + 8 + k, twin)

    def second_far(k, first):
        opposite = slot_at(first, b + 2)
        mover.got(xg.at[0, opposite], B2U + k)
        mover.got(xg.at[1, opposite], B2D + k)
        mover.put(xg.at[:, opposite], xg.at[:, opposite], TWIN + 12 + k, twin)

    second(0, a)
    down, up = z_got(1)
    z_step(2, down, up)
    second(1, a + 3)
    second(2, a + 1)
    down, up = z_got(2)
    z_step(3, down, up)
    second(3, a + 2)
    second_far(0, a)
    down, up = z_got(3)
    z_step(4, down, up)
    o_step(1, z, z)
    second_far(1, a + 3)
    second_far(2, a + 1)
    second_far(3, a + 2)
    opposite = (z + 4) % NZ
    down, up = o_got(1)
    o_step(2, down, up)
    mover.got(wg.at[0, :, opposite], ZW + 6)
    mover.got(wg.at[1, :, opposite], ZW + 7)
    down, up = o_got(2)
    o_step(3, down, up)
    for d in range(1, GROUP):
        mover.got(sgg.at[own_group], s_slot(d))
    for k in range(16):
        mover.got(xg.at[:, own], TWIN + k)
    down, up = o_got(3)
    o_step(4, down, up)
    mover.got(wog.at[0, opposite], ZO + 6)
    mover.got(wog.at[1, opposite], ZO + 7)
    local[1].wait()
    local[3].wait()
    mover.finish()


def project_kernel(x_ref, w_ref, s_ref, gain_ref, keep_ref, y_ref):
    mean_part = jnp.dot(x_ref[0], w_ref[0], preferred_element_type=F32)
    delta_part = jnp.dot(x_ref[1], w_ref[1], preferred_element_type=F32)
    both = (mean_part + s_ref[...].astype(F32) * delta_part).astype(BF16).astype(F32)
    for e in range(2):
        unit = both[:, e * HEAD : (e + 1) * HEAD]
        inverse = lax.rsqrt(jnp.mean(unit * unit, axis=-1, keepdims=True) + EPSILON)
        normed = unit * inverse * gain_ref[e : e + 1, :]
        y_ref[e] = jnp.where(keep_ref[e : e + 1, :] > 0, unit, normed).astype(BF16)


def exchange_kernel(heads, y_ref, kv, q, send, recv, loc):
    x, y, z, c = place()
    me = device(x, y, z, c)
    own = x * 2 + y % 2
    peers = [group_peer(x, y, z, c, d) for d in range(1, GROUP)]
    z_up, z_down = device(x, y, (z + 1) % NZ, c), device(x, y, (z + 7) % NZ, c)
    greet([peer for peer, _ in peers] + [z_up, z_down])
    ref_send, ref_recv = send, recv

    def copy_to(src, dst, s, r, where):
        return pltpu.make_async_remote_copy(
            src_ref=src,
            dst_ref=dst,
            send_sem=ref_send.at[s],
            recv_sem=ref_recv.at[r],
            device_id=where,
            device_id_type=MESH,
        )

    rows = q.shape[2]
    for e in range(2):
        unit = own * 2 + e

        @pl.when(unit < heads)
        def _():
            for d, (peer, there) in enumerate(peers, 1):
                copy_to(
                    y_ref.at[e, pl.ds(there * rows, rows)], q.at[z, unit], e * 7 + d - 1, unit, peer
                ).start()
            pltpu.make_async_copy(
                y_ref.at[e, pl.ds(own * rows, rows)], q.at[z, unit], loc.at[e]
            ).start()

        @pl.when((unit >= heads) & (unit < 3 * heads))
        def _():
            for d, (peer, there) in enumerate(peers, 1):
                copy_to(y_ref.at[e], kv.at[unit - heads], e * 7 + d - 1, unit, peer).start()
            pltpu.make_async_copy(y_ref.at[e], kv.at[unit - heads], loc.at[e]).start()

    for n in range(heads):
        landed = q.at[z, n]

        @pl.when(own == n // 2)
        def _():
            pltpu.make_async_copy(y_ref.at[n % 2, pl.ds(own * rows, rows)], landed, loc.at[n % 2]).wait()

        @pl.when(own != n // 2)
        def _():
            copy_to(landed, landed, 0, n, me).wait_recv()

    Z = 3 * heads
    ring = []
    for t in range(1, 5):
        down, up = (z + 8 - (t - 1)) % NZ, (z + t - 1) % NZ
        if t > 1:
            copy_to(q.at[down], q.at[down], 0, Z + 2 * (t - 2), me).wait_recv()
            copy_to(q.at[up], q.at[up], 0, Z + 2 * (t - 2) + 1, me).wait_recv()
        if t < 4:
            ring.append(copy_to(q.at[down], q.at[down], 14 + 2 * (t - 1), Z + 2 * (t - 1), z_up))
            ring.append(copy_to(q.at[up], q.at[up], 15 + 2 * (t - 1), Z + 2 * (t - 1) + 1, z_down))
        else:
            cut = (heads + 1) // 2
            lower, upper = pl.ds(0, cut), pl.ds(cut, heads - cut)
            ring.append(copy_to(q.at[down, lower], q.at[down, lower], 20, Z + 6, z_up))
            ring.append(copy_to(q.at[up, upper], q.at[up, upper], 21, Z + 7, z_down))
        ring[-2].start()
        ring[-1].start()
    for n in range(heads, 3 * heads):
        landed = kv.at[n - heads]

        @pl.when(own == n // 2)
        def _():
            pltpu.make_async_copy(y_ref.at[n % 2], landed, loc.at[n % 2]).wait()

        @pl.when(own != n // 2)
        def _():
            copy_to(landed, landed, 0, n, me).wait_recv()

    cut = (heads + 1) // 2
    far = (z + 4) % NZ
    lower, upper = pl.ds(0, cut), pl.ds(cut, heads - cut)
    copy_to(q.at[far, lower], q.at[far, lower], 0, Z + 6, me).wait_recv()
    copy_to(q.at[far, upper], q.at[far, upper], 0, Z + 7, me).wait_recv()
    for copy in ring:
        copy.wait_send()
    for e in range(2):
        unit = own * 2 + e

        @pl.when(unit < heads)
        def _():
            for d, (peer, there) in enumerate(peers, 1):
                copy_to(
                    y_ref.at[e, pl.ds(there * rows, rows)], q.at[z, unit], e * 7 + d - 1, unit, peer
                ).wait_send()

        @pl.when((unit >= heads) & (unit < 3 * heads))
        def _():
            for d, (peer, there) in enumerate(peers, 1):
                copy_to(y_ref.at[e], kv.at[unit - heads], e * 7 + d - 1, unit, peer).wait_send()


def attend_kernel(heads, factor, q_ref, k_ref, v_ref, o_ref):
    head = pl.program_id(0)
    planes, rows = q_ref.shape[0], q_ref.shape[2]
    key_block = k_ref[0]
    values = jnp.concatenate([v_ref[0], jnp.ones_like(v_ref[0])], axis=1)
    lane = lax.broadcasted_iota(jnp.int32, (rows, HEAD), 1)

    @pl.when(head == 0)
    def _():
        o_ref[:, :, heads * HEAD :] = jnp.zeros((planes, rows, HEAD), BF16)

    for p in range(planes):
        scores = lax.dot_general(
            q_ref[p, 0], key_block, (((1,), (1,)), ((), ())), preferred_element_type=F32
        )
        weights = jnp.exp2(scores * factor).astype(BF16)
        sums = jnp.dot(weights, values, preferred_element_type=F32)
        o_ref[p, :, pl.ds(pl.multiple_of(head * HEAD, HEAD), HEAD)] = sums[:, :HEAD].astype(BF16)
        held = o_ref[p, :, heads * HEAD :].astype(F32)
        o_ref[p, :, heads * HEAD :] = jnp.where(lane == head, sums[:, HEAD:], held).astype(BF16)


def z_scatter_kernel(part, out, send, recv, loc):
    x, y, z, c = place()
    peers = [(device(x, y, (z + d) % NZ, c), (z + d) % NZ) for d in range(1, NZ)]
    greet([peer for peer, _ in peers])
    mover = Mover(send, recv, device(x, y, z, c))
    local = pltpu.make_async_copy(part.at[z], out.at[z], loc.at[0])
    local.start()
    for d, (peer, there) in enumerate(peers, 1):
        mover.put(part.at[there], out.at[z], d - 1, peer)
    for d in range(1, NZ):
        mover.got(out.at[z], d - 1)
    local.wait()
    mover.finish()


def group_gather_kernel(rows_ref, out, send, recv, loc):
    x, y, z, c = place()
    own = x * 2 + y % 2
    peers = [group_peer(x, y, z, c, d) for d in range(1, GROUP)]
    greet([peer for peer, _ in peers])
    mover = Mover(send, recv, device(x, y, z, c))
    local = pltpu.make_async_copy(rows_ref, out.at[:, own], loc.at[0])
    local.start()
    for d, (peer, there) in enumerate(peers, 1):
        mover.put(rows_ref, out.at[:, own], d - 1, peer)
    for d in range(1, GROUP):
        mover.got(out.at[:, own], d - 1)
    local.wait()
    mover.finish()


def out_kernel(a_ref, w_ref, o_ref):
    for m in range(2):
        o_ref[m] = lax.dot_general(
            a_ref[m], w_ref[m], (((1,), (1,)), ((), ())), preferred_element_type=F32
        ).astype(BF16)


def owner_scatter_kernel(part, out, send, recv, loc):
    x, y, z, c = place()
    own = row_slot(x, y, c)
    count = NX * NY * NC
    peers = []
    for d in range(1, count):
        there = (own + d) % count
        peers.append(
            (device(there // 8, ((there // 2) % 2) * 2 + (there // 4) % 2, z, there % 2), there)
        )
    greet([peer for peer, _ in peers])
    mover = Mover(send, recv, device(x, y, z, c))
    local = pltpu.make_async_copy(part.at[:, own], out.at[:, own], loc.at[0])
    local.start()
    for d, (peer, there) in enumerate(peers, 1):
        mover.put(part.at[:, there], out.at[:, own], d - 1, peer)
    for d in range(1, count):
        mover.got(out.at[:, own], d - 1)
    local.wait()
    mover.finish()


def vmem(count):
    return [pl.BlockSpec(memory_space=pltpu.VMEM)] * count


def body(
    tokens, in_bits, qkv_weights, qkv_bits, gain_query, gain_key, out_weights, mix_bits, out_bits
):
    own_rows, width = tokens.shape
    depth, columns = qkv_weights.shape[2], qkv_weights.shape[3]
    heads = columns // HEAD
    rows = qkv_bits.shape[0]
    plane_rows = rows * GROUP
    blk, uly = lax.axis_index("blk"), lax.axis_index("uly")
    group = (blk // 16) * 2 + blk % 2

    flipped = (tokens.astype(F32) * signed(in_bits)).astype(BF16)
    shard = jnp.stack([tokens, flipped])
    units = jnp.transpose(qkv_weights.reshape(2, 3, depth, heads, HEAD), (1, 3, 0, 2, 4))
    units = units.reshape(3 * heads, 2, depth, HEAD)
    units = jnp.concatenate([units, units[-1:]])
    wj = jnp.transpose(units.reshape(GROUP, 2, 2, depth, HEAD), (0, 2, 3, 1, 4))
    wj = wj.reshape(GROUP, 2, depth, 2 * HEAD)
    wo = jnp.transpose(out_weights, (0, 2, 1))
    signs = signed(qkv_bits).astype(BF16).reshape(rows, 3 * heads * HEAD)
    signs = jnp.concatenate([signs, signs[:, -HEAD:]], axis=1)
    signs = jnp.transpose(signs.reshape(rows, GROUP, 2 * HEAD), (1, 0, 2))

    xg, wg, wog, sgg = comm(
        gather_kernel,
        (shard, wj, wo, signs),
        [
            jax.ShapeDtypeStruct((2, NX * NY * NC, own_rows, width), BF16),
            jax.ShapeDtypeStruct((2, NX, NZ, 2, depth, 2 * HEAD), BF16),
            jax.ShapeDtypeStruct((2, NZ) + wo.shape[1:], BF16),
            jax.ShapeDtypeStruct((GROUP, rows, 2 * HEAD), BF16),
        ],
        66,
        66,
        4,
        0,
    )

    gains = jnp.concatenate(
        [gain_query.reshape(heads, HEAD), gain_key.reshape(heads, HEAD), jnp.ones((heads + 1, HEAD), F32)]
    )
    gain = lax.dynamic_slice_in_dim(gains, group * 2, 2, 0)
    keep = (group * 2 + jnp.arange(2) >= 2 * heads).astype(F32)[:, None] * jnp.ones((1, HEAD), F32)

    step = 128
    y = pl.pallas_call(
        project_kernel,
        grid=(plane_rows // step,),
        out_shape=jax.ShapeDtypeStruct((2, plane_rows, HEAD), BF16),
        in_specs=[
            pl.BlockSpec((2, step, width), lambda i: (0, i, 0)),
            pl.BlockSpec((2, width, 2 * HEAD), lambda i: (0, 0, 0)),
            pl.BlockSpec((step, 2 * HEAD), lambda i: (i, 0)),
            pl.BlockSpec((2, HEAD), lambda i: (0, 0)),
            pl.BlockSpec((2, HEAD), lambda i: (0, 0)),
        ],
        out_specs=pl.BlockSpec((2, step, HEAD), lambda i: (0, i, 0)),
        compiler_params=pltpu.CompilerParams(vmem_limit_bytes=40 << 20),
    )(
        xg.reshape(2, plane_rows, width),
        wg.reshape(2, width, 2 * HEAD),
        sgg.reshape(plane_rows, 2 * HEAD),
        gain,
        keep,
    )

    kv, q = comm(
        functools.partial(exchange_kernel, heads),
        (y,),
        [
            jax.ShapeDtypeStruct((2 * heads, plane_rows, HEAD), BF16),
            jax.ShapeDtypeStruct((NZ, heads, rows, HEAD), BF16),
        ],
        22,
        3 * heads + 8,
        2,
        1,
    )

    packed = (heads + 1) * HEAD
    part = pl.pallas_call(
        functools.partial(attend_kernel, heads, math.log2(math.e) / math.sqrt(HEAD)),
        grid=(heads,),
        out_shape=jax.ShapeDtypeStruct((NZ, rows, packed), BF16),
        in_specs=[
            pl.BlockSpec((NZ, 1, rows, HEAD), lambda i: (0, i, 0, 0)),
            pl.BlockSpec((1, plane_rows, HEAD), lambda i: (i, 0, 0)),
            pl.BlockSpec((1, plane_rows, HEAD), lambda i: (i + heads, 0, 0)),
        ],
        out_specs=pl.BlockSpec((NZ, rows, packed), lambda i: (0, 0, 0)),
        compiler_params=pltpu.CompilerParams(vmem_limit_bytes=40 << 20),
    )(q, kv, kv)

    (parts,) = comm(z_scatter_kernel, (part,), [jax.ShapeDtypeStruct(part.shape, BF16)], 7, 7, 1, 2)
    sums = jnp.sum(parts.astype(F32), axis=0)
    numerator = sums[:, : heads * HEAD].reshape(rows, heads, HEAD)
    denominator = sums[:, heads * HEAD : heads * HEAD + heads]
    attended = (numerator / denominator[:, :, None]).astype(BF16).reshape(rows, heads * HEAD)
    attended_flipped = (attended.astype(F32) * signed(mix_bits)).astype(BF16)
    pair = jnp.stack([attended, attended_flipped])

    (pairs,) = comm(
        group_gather_kernel,
        (pair,),
        [jax.ShapeDtypeStruct((2, GROUP) + pair.shape[1:], BF16)],
        7,
        7,
        1,
        3,
    )
    out_columns = NZ * wo.shape[1]
    partial_out = pl.pallas_call(
        out_kernel,
        out_shape=jax.ShapeDtypeStruct((2, plane_rows, out_columns), BF16),
        in_specs=vmem(2),
        out_specs=pl.BlockSpec(memory_space=pltpu.VMEM),
        compiler_params=pltpu.CompilerParams(vmem_limit_bytes=40 << 20),
    )(pairs.reshape(2, plane_rows, columns), wog.reshape(2, out_columns, columns))

    count = NX * NY * NC
    (landed,) = comm(
        owner_scatter_kernel,
        (partial_out.reshape(2, count, own_rows, out_columns),),
        [jax.ShapeDtypeStruct((2, count, own_rows, out_columns), BF16)],
        count - 1,
        count - 1,
        1,
        4,
    )
    summed = jnp.sum(landed.astype(F32).reshape(2, GROUP, 4, own_rows, out_columns), axis=2)
    summed = summed.reshape(2, NX, 2, own_rows, NZ, out_columns // NZ)
    summed = jnp.transpose(summed, (0, 3, 1, 4, 2, 5)).reshape(2, own_rows, width)
    own_bits = lax.dynamic_slice_in_dim(out_bits, uly * own_rows, own_rows, 0)
    return (summed[0] + signed(own_bits) * summed[1]).astype(BF16)


def solution(mesh):
    return jax.shard_map(
        body,
        mesh=mesh,
        in_specs=(
            P(("blk", "uly"), None),
            P(("blk", "uly"), None),
            P(None, None, "blk", "uly"),
            P("blk", None, "uly"),
            P("uly"),
            P("uly"),
            P(None, "uly", "blk"),
            P("blk", "uly"),
            P("blk", None),
        ),
        out_specs=P(("blk", "uly"), None),
        check_vma=False,
    )
```

```python
import functools
import math

import jax
import jax.numpy as jnp
from jax import lax
from jax.experimental import pallas as pl
from jax.experimental.pallas import tpu as pltpu
from jax.sharding import PartitionSpec as P

HEAD = 128
NX, NY, NZ, NC = 4, 4, 8, 2
GROUP = 8
EPSILON = 1e-06
MESH = pl.DeviceIdType.MESH
BF16 = jnp.bfloat16
F32 = jnp.float32


def signed(bits):
    return (2 * bits - 1).astype(F32)


def place():
    blk, uly = lax.axis_index("blk"), lax.axis_index("uly")
    return blk // 16, (uly // 2) * 2 + blk % 2, (blk // 2) % 8, uly % 2


def device(x, y, z, c):
    return {"blk": x * 16 + z * 2 + y % 2, "uly": (y // 2) * 2 + c}


def row_slot(x, y, c):
    return x * 8 + (y % 2) * 4 + (y // 2) * 2 + c


class Mover:
    def __init__(self, send, recv, me):
        self.send, self.recv, self.me, self.sent = send, recv, me, []

    def put(self, src, dst, slot, where):
        copy = pltpu.make_async_remote_copy(
            src_ref=src,
            dst_ref=dst,
            send_sem=self.send.at[len(self.sent)],
            recv_sem=self.recv.at[slot],
            device_id=where,
            device_id_type=MESH,
        )
        copy.start()
        self.sent.append(copy)

    def got(self, ref, slot):
        pltpu.make_async_remote_copy(
            src_ref=ref,
            dst_ref=ref,
            send_sem=self.send.at[0],
            recv_sem=self.recv.at[slot],
            device_id=self.me,
            device_id_type=MESH,
        ).wait_recv()

    def finish(self):
        for copy in self.sent:
            copy.wait_send()


def greet(sources, count):
    barrier = pltpu.get_barrier_semaphore()
    for source in sources:
        pl.semaphore_signal(barrier, inc=1, device_id=source, device_id_type=MESH)
    pl.semaphore_wait(barrier, count)


def group_peer(x, y, z, c, d):
    there = (x * 2 + c + d) % GROUP
    return device(there // 2, y, z, there % 2), there


def comm(kernel, args, outs, sends, recvs, locals_, collective_id):
    return pl.pallas_call(
        kernel,
        out_shape=outs,
        in_specs=[pl.BlockSpec(memory_space=pl.ANY)] * len(args),
        out_specs=[pl.BlockSpec(memory_space=pl.ANY)] * len(outs),
        scratch_shapes=[
            pltpu.SemaphoreType.DMA((sends,)),
            pltpu.SemaphoreType.DMA((recvs,)),
            pltpu.SemaphoreType.DMA((locals_,)),
        ],
        compiler_params=pltpu.CompilerParams(collective_id=collective_id, has_side_effects=True),
    )(*args)


def gather_kernel(xs, wj, sg, gains, xg, wg, sgg, gg, send, recv, loc):
    x, y, z, c = place()
    low, high = y % 2, y // 2
    me = device(x, y, z, c)
    group = x * 2 + c
    chunk = x * 2 + low
    a = x * (1 - c) + y * c
    b = y * (1 - c) + x * c

    def at(first, second):
        return first * (1 - c) + second * c, second * (1 - c) + first * c

    def dev_at(first, second):
        px, py = at(first % 4, second % 4)
        return device(px, py, z, c)

    def slot_at(first, second):
        px, py = at(first % 4, second % 4)
        return row_slot(px, py, c)

    a_up, a_down = dev_at(a + 1, b), dev_at(a + 3, b)
    b_up, b_down = dev_at(a, b + 1), dev_at(a, b + 3)
    z_up, z_down = device(x, y, (z + 1) % NZ, c), device(x, y, (z + 7) % NZ, c)
    twin = device(x, y, z, 1 - c)
    targets = []
    for d in range(GROUP):
        there = (group + d) % GROUP
        targets.append((device(there // 2, high * 2 + c, z, there % 2), there))
    origins = [device(k // 2, high * 2 + k % 2, z, low) for k in range(GROUP)]
    stays = low == c

    barrier = pltpu.get_barrier_semaphore()
    for near in (a_up, a_down, b_up, b_down, z_up, z_down, twin):
        pl.semaphore_signal(barrier, inc=1, device_id=near, device_id_type=MESH)
    for k, origin in enumerate(origins):

        @pl.when(jnp.logical_not(stays & (chunk == k)))
        def _():
            pl.semaphore_signal(barrier, inc=1, device_id=origin, device_id_type=MESH)

    @pl.when(stays)
    def _():
        pl.semaphore_wait(barrier, 7 + GROUP - 1)

    @pl.when(jnp.logical_not(stays))
    def _():
        pl.semaphore_wait(barrier, 7 + GROUP)

    mover = Mover(send, recv, me)
    own = slot_at(a, b)
    A1, A2, B1U, B1D, B2U, B2D, TWIN, ZW, GAIN, SIGN = 8, 10, 12, 16, 20, 24, 28, 44, 52, 53
    KEPT = 59

    def kept(part, remote):
        source = wj.at[group] if part == 0 else sg.at[group]
        landed = wg.at[:, x, z, low] if part == 0 else sgg.at[chunk]
        if not remote:
            return pltpu.make_async_copy(source, landed, loc.at[part])
        return pltpu.make_async_remote_copy(
            src_ref=source,
            dst_ref=landed,
            send_sem=send.at[KEPT + part],
            recv_sem=recv.at[chunk + SIGN * part],
            device_id=targets[0][0],
            device_id_type=MESH,
        )

    def start_kept(part):
        @pl.when(stays)
        def _():
            kept(part, False).start()

        @pl.when(jnp.logical_not(stays))
        def _():
            kept(part, True).start()

    def arrive_all(part, ref):
        for k in range(GROUP):
            mine = stays & (chunk == k)

            @pl.when(mine)
            def _():
                kept(part, False).wait()

            @pl.when(jnp.logical_not(mine))
            def _():
                mover.got(ref, k + SIGN * part)

    start_kept(0)
    for peer, there in targets[1:]:
        mover.put(wj.at[there], wg.at[:, x, z, low], chunk, peer)
    mover.put(xs, xg.at[:, own], A1, a_up)
    mover.put(xs, xg.at[:, own], A1 + 1, a_down)
    mover.put(xs, xg.at[:, own], B1U, b_up)
    mover.put(xs, xg.at[:, own], B1D, b_down)
    mover.put(xs, xg.at[:, own], TWIN, twin)
    mover.put(gains, gg.at[c], GAIN, twin)
    own_rows = pltpu.make_async_copy(xs, xg.at[:, own], loc.at[2])
    own_gains = pltpu.make_async_copy(gains, gg.at[c], loc.at[3])
    own_rows.start()
    own_gains.start()
    start_kept(1)
    for peer, there in targets[1:]:
        mover.put(sg.at[there], sgg.at[chunk], SIGN + chunk, peer)

    arrive_all(0, wg.at[:, x, z, low])

    def z_step(t, source_down, source_up):
        if t < 4:
            mover.put(wg.at[:, :, source_down], wg.at[:, :, source_down], ZW + 2 * (t - 1), z_up)
            mover.put(wg.at[:, :, source_up], wg.at[:, :, source_up], ZW + 2 * (t - 1) + 1, z_down)
        else:
            mover.put(wg.at[0, :, source_down], wg.at[0, :, source_down], ZW + 6, z_up)
            mover.put(wg.at[1, :, source_up], wg.at[1, :, source_up], ZW + 7, z_down)

    def z_got(t):
        down, up = (z + 8 - t) % NZ, (z + t) % NZ
        mover.got(wg.at[:, :, down], ZW + 2 * (t - 1))
        mover.got(wg.at[:, :, up], ZW + 2 * (t - 1) + 1)
        return down, up

    z_step(1, z, z)

    def spread(slot, k):
        shard = xg.at[:, slot]
        mover.put(shard, shard, B1U + k, b_up)
        mover.put(shard, shard, B1D + k, b_down)
        mover.put(shard, shard, TWIN + k, twin)

    from_down, from_up, far = slot_at(a + 3, b), slot_at(a + 1, b), slot_at(a + 2, b)
    mover.got(xg.at[:, from_down], A1)
    mover.put(xg.at[0, from_down], xg.at[0, from_down], A2, a_up)
    spread(from_down, 1)
    mover.got(xg.at[:, from_up], A1 + 1)
    mover.put(xg.at[1, from_up], xg.at[1, from_up], A2 + 1, a_down)
    spread(from_up, 2)
    mover.got(xg.at[0, far], A2)
    mover.got(xg.at[1, far], A2 + 1)
    spread(far, 3)

    def second(k, first):
        down, up = slot_at(first, b + 3), slot_at(first, b + 1)
        mover.got(xg.at[:, down], B1U + k)
        mover.put(xg.at[0, down], xg.at[0, down], B2U + k, b_up)
        mover.put(xg.at[:, down], xg.at[:, down], TWIN + 4 + k, twin)
        mover.got(xg.at[:, up], B1D + k)
        mover.put(xg.at[1, up], xg.at[1, up], B2D + k, b_down)
        mover.put(xg.at[:, up], xg.at[:, up], TWIN + 8 + k, twin)

    def second_far(k, first):
        opposite = slot_at(first, b + 2)
        mover.got(xg.at[0, opposite], B2U + k)
        mover.got(xg.at[1, opposite], B2D + k)
        mover.put(xg.at[:, opposite], xg.at[:, opposite], TWIN + 12 + k, twin)

    second(0, a)
    down, up = z_got(1)
    z_step(2, down, up)
    second(1, a + 3)
    second(2, a + 1)
    down, up = z_got(2)
    z_step(3, down, up)
    second(3, a + 2)
    second_far(0, a)
    second_far(1, a + 3)
    down, up = z_got(3)
    z_step(4, down, up)
    second_far(2, a + 1)
    second_far(3, a + 2)
    opposite = (z + 4) % NZ
    arrive_all(1, sgg.at[chunk])
    for k in range(16):
        mover.got(xg.at[:, own], TWIN + k)
    mover.got(gg.at[c], GAIN)
    mover.got(wg.at[0, :, opposite], ZW + 6)
    mover.got(wg.at[1, :, opposite], ZW + 7)
    own_rows.wait()
    own_gains.wait()
    assert len(mover.sent) == KEPT, len(mover.sent)
    mover.finish()

    @pl.when(jnp.logical_not(stays))
    def _():
        for part in range(2):
            kept(part, True).wait_send()


def project_kernel(x_ref, w_ref, s_ref, gain_ref, keep_ref, y_ref):
    mean_part = jnp.dot(x_ref[0], w_ref[0], preferred_element_type=F32)
    delta_part = jnp.dot(x_ref[1], w_ref[1], preferred_element_type=F32)
    both = (mean_part + s_ref[...].astype(F32) * delta_part).astype(BF16).astype(F32)
    for e in range(2):
        unit = both[:, e * HEAD : (e + 1) * HEAD]
        inverse = lax.rsqrt(jnp.mean(unit * unit, axis=-1, keepdims=True) + EPSILON)
        normed = unit * inverse * gain_ref[e : e + 1, :]
        y_ref[e] = jnp.where(keep_ref[e : e + 1, :] > 0, unit, normed).astype(BF16)


def exchange_kernel(heads, y_ref, mix, wo, kv, q, mixed, wos, send, recv, loc):
    x, y, z, c = place()
    low, high = y % 2, y // 2
    me = device(x, y, z, c)
    own = x * 2 + c
    rows = q.shape[2]
    units = 3 * heads
    peers = [group_peer(x, y, z, c, d) for d in range(1, GROUP)]
    aligned = [device((x + d) % NX, y, z, c) for d in range(1, NX)]
    twin = device(x, y, z, 1 - c)
    swap = device(x, high * 2 + c, z, low)
    z_up, z_down = device(x, y, (z + 1) % NZ, c), device(x, y, (z + 7) % NZ, c)
    moves = low != c

    barrier = pltpu.get_barrier_semaphore()
    for near in [peer for peer, _ in peers] + [z_up, z_down]:
        pl.semaphore_signal(barrier, inc=1, device_id=near, device_id_type=MESH)

    @pl.when(moves)
    def _():
        pl.semaphore_signal(barrier, inc=1, device_id=swap, device_id_type=MESH)
        pl.semaphore_wait(barrier, GROUP + 2)

    @pl.when(jnp.logical_not(moves))
    def _():
        pl.semaphore_wait(barrier, GROUP + 1)

    def copy_to(src, dst, s, r, where):
        return pltpu.make_async_remote_copy(
            src_ref=src,
            dst_ref=dst,
            send_sem=send.at[s],
            recv_sem=recv.at[r],
            device_id=where,
            device_id_type=MESH,
        )

    RING, FORWARD = 14, 22
    SWAP = FORWARD + 2 * heads
    Z, R_SWAP = units, units + 8

    def own_copies(n):
        e = n % 2
        if n < heads:
            return [
                copy_to(y_ref.at[e, pl.ds(there * rows, rows)], q.at[z, n], e * 7 + d, n, peer)
                for d, (peer, there) in enumerate(peers)
            ]
        landed = kv.at[n - heads]
        return [
            copy_to(y_ref.at[e], landed, e * 7 + d, n, peer)
            for d, peer in enumerate(aligned + [twin])
        ]

    def kept(n):
        source = y_ref.at[n % 2]
        if n < heads:
            return pltpu.make_async_copy(source.at[pl.ds(own * rows, rows)], q.at[z, n], loc.at[n % 2])
        return pltpu.make_async_copy(source, kv.at[n - heads], loc.at[n % 2])

    for n in range(units):

        @pl.when(own == n // 2)
        def _():
            for copy in own_copies(n):
                copy.start()
            kept(n).start()

    swaps = [copy_to(mix, mixed, SWAP, R_SWAP, swap), copy_to(wo, wos, SWAP + 1, R_SWAP + 1, swap)]
    stays = [
        pltpu.make_async_copy(mix, mixed, loc.at[2]),
        pltpu.make_async_copy(wo, wos, loc.at[3]),
    ]

    @pl.when(moves)
    def _():
        for copy in swaps:
            copy.start()

    @pl.when(jnp.logical_not(moves))
    def _():
        for copy in stays:
            copy.start()

    def arrive(n):
        landed = q.at[z, n] if n < heads else kv.at[n - heads]

        @pl.when(own == n // 2)
        def _():
            kept(n).wait()

        @pl.when(own != n // 2)
        def _():
            copy_to(landed, landed, 0, n, me).wait_recv()

    def forward(n):
        landed = kv.at[n - heads]
        return copy_to(landed, landed, FORWARD + n - heads, n, twin)

    def forwards(n):
        return (own != n // 2) & (c == (n // 2) % 2)

    for n in range(heads):
        arrive(n)

    cut = (heads + 1) // 2
    lower, upper = pl.ds(0, cut), pl.ds(cut, heads - cut)
    ring = []

    def ring_step(t):
        down, up = (z + 8 - (t - 1)) % NZ, (z + t - 1) % NZ
        if t > 1:
            copy_to(q.at[down], q.at[down], 0, Z + 2 * (t - 2), me).wait_recv()
            copy_to(q.at[up], q.at[up], 0, Z + 2 * (t - 2) + 1, me).wait_recv()
        r, s = Z + 2 * (t - 1), RING + 2 * (t - 1)
        if t < 4:
            ring.append(copy_to(q.at[down], q.at[down], s, r, z_up))
            ring.append(copy_to(q.at[up], q.at[up], s + 1, r + 1, z_down))
        else:
            ring.append(copy_to(q.at[down, lower], q.at[down, lower], s, r, z_up))
            ring.append(copy_to(q.at[up, upper], q.at[up, upper], s + 1, r + 1, z_down))
        ring[-2].start()
        ring[-1].start()

    ring_step(1)
    for t in range(2, 5):
        ring_step(t)
        for n in range(heads, units):
            if (n - heads) % 3 == t - 2:
                arrive(n)

                @pl.when(forwards(n))
                def _():
                    forward(n).start()

    far = (z + 4) % NZ
    copy_to(q.at[far, lower], q.at[far, lower], 0, Z + 6, me).wait_recv()
    copy_to(q.at[far, upper], q.at[far, upper], 0, Z + 7, me).wait_recv()
    for copy in ring:
        copy.wait_send()
    for n in range(units):

        @pl.when(own == n // 2)
        def _():
            for copy in own_copies(n):
                copy.wait_send()

        if n >= heads:

            @pl.when(forwards(n))
            def _():
                forward(n).wait_send()

    @pl.when(moves)
    def _():
        for copy in swaps:
            copy.wait()

    @pl.when(jnp.logical_not(moves))
    def _():
        for copy in stays:
            copy.wait()


def attend_kernel(heads, factor, q_ref, k_ref, v_ref, o_ref):
    head = pl.program_id(0)
    planes, rows = q_ref.shape[0], q_ref.shape[2]
    key_block = k_ref[0]
    values = jnp.concatenate([v_ref[0], jnp.ones_like(v_ref[0])], axis=1)
    lane = lax.broadcasted_iota(jnp.int32, (rows, HEAD), 1)

    @pl.when(head == 0)
    def _():
        o_ref[:, :, heads * HEAD :] = jnp.zeros((planes, rows, HEAD), BF16)

    for p in range(planes):
        scores = lax.dot_general(
            q_ref[p, 0], key_block, (((1,), (1,)), ((), ())), preferred_element_type=F32
        )
        weights = jnp.exp2(scores * factor).astype(BF16)
        sums = jnp.dot(weights, values, preferred_element_type=F32)
        o_ref[p, :, pl.ds(pl.multiple_of(head * HEAD, HEAD), HEAD)] = sums[:, :HEAD].astype(BF16)
        held = o_ref[p, :, heads * HEAD :].astype(F32)
        o_ref[p, :, heads * HEAD :] = jnp.where(lane == head, sums[:, HEAD:], held).astype(BF16)


def z_scatter_kernel(part, out, send, recv, loc):
    x, y, z, c = place()
    peers = [(device(x, y, (z + d) % NZ, c), (z + d) % NZ) for d in range(1, NZ)]
    greet([peer for peer, _ in peers], len(peers))
    mover = Mover(send, recv, device(x, y, z, c))
    local = pltpu.make_async_copy(part.at[z], out.at[z], loc.at[0])
    local.start()
    for d, (peer, there) in enumerate(peers, 1):
        mover.put(part.at[there], out.at[z], d - 1, peer)
    for d in range(1, NZ):
        mover.got(out.at[z], d - 1)
    local.wait()
    mover.finish()


def group_gather_kernel(rows_ref, wo, out, wog, send, recv, loc):
    x, y, z, c = place()
    own = x * 2 + c
    aligned = [device((x + d) % NX, y, z, c) for d in range(1, NX)]
    twin = device(x, y, z, 1 - c)
    z_up, z_down = device(x, y, (z + 1) % NZ, c), device(x, y, (z + 7) % NZ, c)
    near = aligned + [twin, z_up, z_down]
    greet(near, len(near))
    mover = Mover(send, recv, device(x, y, z, c))
    local = [
        pltpu.make_async_copy(rows_ref, out.at[:, own], loc.at[0]),
        pltpu.make_async_copy(wo, wog.at[:, z], loc.at[1]),
    ]
    for copy in local:
        copy.start()
    TWIN, ZO = 3, 7
    for d, peer in enumerate(aligned):
        mover.put(rows_ref, out.at[:, own], d, peer)
    mover.put(rows_ref, out.at[:, own], TWIN, twin)
    mover.put(wo, wog.at[:, z], ZO, z_up)
    mover.put(wo, wog.at[:, z], ZO + 1, z_down)

    def o_next(t):
        down, up = (z + 8 - t) % NZ, (z + t) % NZ
        mover.got(wog.at[:, down], ZO + 2 * (t - 1))
        mover.got(wog.at[:, up], ZO + 2 * (t - 1) + 1)
        if t < 3:
            mover.put(wog.at[:, down], wog.at[:, down], ZO + 2 * t, z_up)
            mover.put(wog.at[:, up], wog.at[:, up], ZO + 2 * t + 1, z_down)
        else:
            mover.put(wog.at[0, down], wog.at[0, down], ZO + 6, z_up)
            mover.put(wog.at[1, up], wog.at[1, up], ZO + 7, z_down)

    order = (0, 2, 1)
    o_next(1)
    for step, d in enumerate(order):
        there = ((x + NX - 1 - d) % NX) * 2 + c
        mover.got(out.at[:, there], d)
        mover.put(out.at[:, there], out.at[:, there], TWIN + 1 + d, twin)
        if step < 2:
            o_next(2 + step)
    far = (z + 4) % NZ
    mover.got(wog.at[0, far], ZO + 6)
    mover.got(wog.at[1, far], ZO + 7)
    for k in range(NX):
        mover.got(out.at[:, own], TWIN + k)
    for copy in local:
        copy.wait()
    mover.finish()


def out_kernel(a_ref, w_ref, o_ref):
    for m in range(2):
        o_ref[m] = lax.dot_general(
            a_ref[m], w_ref[m], (((1,), (1,)), ((), ())), preferred_element_type=F32
        ).astype(BF16)


def owner_scatter_kernel(part, out, send, recv, loc):
    x, y, z, c = place()
    own = row_slot(x, y, c)
    landing = (x * 2 + c) * NY + y
    count = NX * NY * NC
    peers = []
    for d in range(1, count):
        there = (own + d) % count
        peers.append(
            (device(there // 8, ((there // 2) % 2) * 2 + (there // 4) % 2, z, there % 2), there)
        )
    greet([peer for peer, _ in peers], len(peers))
    mover = Mover(send, recv, device(x, y, z, c))
    local = pltpu.make_async_copy(part.at[:, own], out.at[:, landing], loc.at[0])
    local.start()
    for d, (peer, there) in enumerate(peers, 1):
        mover.put(part.at[:, there], out.at[:, landing], d - 1, peer)
    for d in range(1, count):
        mover.got(out.at[:, landing], d - 1)
    local.wait()
    mover.finish()


def vmem(count):
    return [pl.BlockSpec(memory_space=pltpu.VMEM)] * count


def body(
    tokens, in_bits, qkv_weights, qkv_bits, gain_query, gain_key, out_weights, mix_bits, out_bits
):
    own_rows, width = tokens.shape
    depth, columns = qkv_weights.shape[2], qkv_weights.shape[3]
    heads = columns // HEAD
    rows = qkv_bits.shape[0]
    plane_rows = rows * GROUP
    x, y, _, c = place()
    group = x * 2 + c

    flipped = (tokens.astype(F32) * signed(in_bits)).astype(BF16)
    shard = jnp.stack([tokens, flipped])
    units = jnp.transpose(qkv_weights.reshape(2, 3, depth, heads, HEAD), (1, 3, 0, 2, 4))
    units = units.reshape(3 * heads, 2, depth, HEAD)
    units = jnp.concatenate([units, units[-1:]])
    wj = jnp.transpose(units.reshape(GROUP, 2, 2, depth, HEAD), (0, 2, 3, 1, 4))
    wj = wj.reshape(GROUP, 2, depth, 2 * HEAD)
    wo = jnp.transpose(out_weights, (0, 2, 1))
    signs = signed(qkv_bits).astype(BF16).reshape(rows, 3 * heads * HEAD)
    signs = jnp.concatenate([signs, signs[:, -HEAD:]], axis=1)
    signs = jnp.transpose(signs.reshape(rows, GROUP, 2 * HEAD), (1, 0, 2))

    gains = jnp.stack([gain_query.reshape(heads, HEAD), gain_key.reshape(heads, HEAD)])

    xg, wg, sgg, gg = comm(
        gather_kernel,
        (shard, wj, signs, gains),
        [
            jax.ShapeDtypeStruct((2, NX * NY * NC, own_rows, width), BF16),
            jax.ShapeDtypeStruct((2, NX, NZ, 2, depth, 2 * HEAD), BF16),
            jax.ShapeDtypeStruct((GROUP, rows, 2 * HEAD), BF16),
            jax.ShapeDtypeStruct((2,) + gains.shape, F32),
        ],
        61,
        61,
        4,
        0,
    )

    gains = lax.dynamic_index_in_dim(gg, y % 2, 0, keepdims=False).reshape(2 * heads, HEAD)
    gains = jnp.concatenate([gains, jnp.ones((heads + 1, HEAD), F32)])
    gain = lax.dynamic_slice_in_dim(gains, group * 2, 2, 0)
    keep = (group * 2 + jnp.arange(2) >= 2 * heads).astype(F32)[:, None] * jnp.ones((1, HEAD), F32)

    step = 128
    units = pl.pallas_call(
        project_kernel,
        grid=(plane_rows // step,),
        out_shape=jax.ShapeDtypeStruct((2, plane_rows, HEAD), BF16),
        in_specs=[
            pl.BlockSpec((2, step, width), lambda i: (0, i, 0)),
            pl.BlockSpec((2, width, 2 * HEAD), lambda i: (0, 0, 0)),
            pl.BlockSpec((step, 2 * HEAD), lambda i: (i, 0)),
            pl.BlockSpec((2, HEAD), lambda i: (0, 0)),
            pl.BlockSpec((2, HEAD), lambda i: (0, 0)),
        ],
        out_specs=pl.BlockSpec((2, step, HEAD), lambda i: (0, i, 0)),
        compiler_params=pltpu.CompilerParams(vmem_limit_bytes=40 << 20),
    )(
        xg.reshape(2, plane_rows, width),
        wg.reshape(2, width, 2 * HEAD),
        sgg.reshape(plane_rows, 2 * HEAD),
        gain,
        keep,
    )

    mix = signed(mix_bits).astype(BF16)
    kv, q, mixed, wo = comm(
        functools.partial(exchange_kernel, heads),
        (units, mix, wo),
        [
            jax.ShapeDtypeStruct((2 * heads, plane_rows, HEAD), BF16),
            jax.ShapeDtypeStruct((NZ, heads, rows, HEAD), BF16),
            jax.ShapeDtypeStruct(mix.shape, BF16),
            jax.ShapeDtypeStruct(wo.shape, BF16),
        ],
        24 + 2 * heads,
        3 * heads + 10,
        4,
        1,
    )

    packed = (heads + 1) * HEAD
    part = pl.pallas_call(
        functools.partial(attend_kernel, heads, math.log2(math.e) / math.sqrt(HEAD)),
        grid=(heads,),
        out_shape=jax.ShapeDtypeStruct((NZ, rows, packed), BF16),
        in_specs=[
            pl.BlockSpec((NZ, 1, rows, HEAD), lambda i: (0, i, 0, 0)),
            pl.BlockSpec((1, plane_rows, HEAD), lambda i: (i, 0, 0)),
            pl.BlockSpec((1, plane_rows, HEAD), lambda i: (i + heads, 0, 0)),
        ],
        out_specs=pl.BlockSpec((NZ, rows, packed), lambda i: (0, 0, 0)),
        compiler_params=pltpu.CompilerParams(vmem_limit_bytes=40 << 20),
    )(q, kv, kv)

    (parts,) = comm(z_scatter_kernel, (part,), [jax.ShapeDtypeStruct(part.shape, BF16)], 7, 7, 1, 2)
    sums = jnp.sum(parts.astype(F32), axis=0)
    numerator = sums[:, : heads * HEAD].reshape(rows, heads, HEAD)
    denominator = sums[:, heads * HEAD : heads * HEAD + heads]
    attended = (numerator / denominator[:, :, None]).astype(BF16).reshape(rows, heads * HEAD)
    attended_flipped = (attended.astype(F32) * mixed.astype(F32)).astype(BF16)
    pair = jnp.stack([attended, attended_flipped])

    pairs, wog = comm(
        group_gather_kernel,
        (pair, wo),
        [
            jax.ShapeDtypeStruct((2, GROUP) + pair.shape[1:], BF16),
            jax.ShapeDtypeStruct((2, NZ) + wo.shape[1:], BF16),
        ],
        15,
        15,
        2,
        3,
    )
    out_columns = NZ * wo.shape[1]
    partial_out = pl.pallas_call(
        out_kernel,
        out_shape=jax.ShapeDtypeStruct((2, plane_rows, out_columns), BF16),
        in_specs=vmem(2),
        out_specs=pl.BlockSpec(memory_space=pltpu.VMEM),
        compiler_params=pltpu.CompilerParams(vmem_limit_bytes=40 << 20),
    )(pairs.reshape(2, plane_rows, columns), wog.reshape(2, out_columns, columns))

    count = NX * NY * NC
    (landed,) = comm(
        owner_scatter_kernel,
        (partial_out.reshape(2, count, own_rows, out_columns),),
        [jax.ShapeDtypeStruct((2, count, own_rows, out_columns), BF16)],
        count - 1,
        count - 1,
        1,
        4,
    )
    summed = jnp.sum(landed.astype(F32).reshape(2, GROUP, 4, own_rows, out_columns), axis=2)
    summed = summed.reshape(2, NX, 2, own_rows, NZ, out_columns // NZ)
    summed = jnp.transpose(summed, (0, 3, 1, 4, 2, 5)).reshape(2, own_rows, width)
    own_bits = lax.dynamic_slice_in_dim(out_bits, lax.axis_index("uly") * own_rows, own_rows, 0)
    return (summed[0] + signed(own_bits) * summed[1]).astype(BF16)


def solution(mesh):
    return jax.shard_map(
        body,
        mesh=mesh,
        in_specs=(
            P(("blk", "uly"), None),
            P(("blk", "uly"), None),
            P(None, None, "blk", "uly"),
            P("blk", None, "uly"),
            P("uly"),
            P("uly"),
            P(None, "uly", "blk"),
            P("blk", "uly"),
            P("blk", None),
        ),
        out_specs=P(("blk", "uly"), None),
        check_vma=False,
    )
```

```python
import functools
import math

import jax
import jax.numpy as jnp
from jax import lax
from jax.experimental import pallas as pl
from jax.experimental.pallas import tpu as pltpu
from jax.sharding import PartitionSpec as P

HEAD = 128
NX, NY, NZ, NC = 4, 4, 8, 2
GROUP = 8
EPSILON = 1e-06
VMEM_LIMIT = 60 << 20
MESH = pl.DeviceIdType.MESH
BF16 = jnp.bfloat16
F32 = jnp.float32


def signed(bits):
    return (2 * bits - 1).astype(F32)


def place():
    blk, uly = lax.axis_index("blk"), lax.axis_index("uly")
    return blk // 16, (uly // 2) * 2 + blk % 2, (blk // 2) % 8, uly % 2


def device(x, y, z, c):
    return {"blk": x * 16 + z * 2 + y % 2, "uly": (y // 2) * 2 + c}


def row_slot(x, y, c):
    return x * 8 + (y % 2) * 4 + (y // 2) * 2 + c


class Mover:
    def __init__(self, send, recv, me, first=0):
        self.send, self.recv, self.me, self.first, self.sent = send, recv, me, first, []

    def put(self, src, dst, slot, where):
        copy = pltpu.make_async_remote_copy(
            src_ref=src,
            dst_ref=dst,
            send_sem=self.send.at[self.first + len(self.sent)],
            recv_sem=self.recv.at[slot],
            device_id=where,
            device_id_type=MESH,
        )
        copy.start()
        self.sent.append(copy)

    def got(self, ref, slot):
        pltpu.make_async_remote_copy(
            src_ref=ref,
            dst_ref=ref,
            send_sem=self.send.at[0],
            recv_sem=self.recv.at[slot],
            device_id=self.me,
            device_id_type=MESH,
        ).wait_recv()

    def finish(self):
        for copy in self.sent:
            copy.wait_send()


def greet(sources, count):
    barrier = pltpu.get_barrier_semaphore()
    for source in sources:
        pl.semaphore_signal(barrier, inc=1, device_id=source, device_id_type=MESH)
    pl.semaphore_wait(barrier, count)


def group_peer(x, y, z, c, d):
    there = (x * 2 + c + d) % GROUP
    return device(there // 2, y, z, there % 2), there


def comm(kernel, args, outs, sends, recvs, locals_, collective_id, scratch=()):
    return pl.pallas_call(
        kernel,
        out_shape=outs,
        in_specs=[pl.BlockSpec(memory_space=pl.ANY)] * len(args),
        out_specs=[pl.BlockSpec(memory_space=pl.ANY)] * len(outs),
        scratch_shapes=list(scratch)
        + [
            pltpu.SemaphoreType.DMA((sends,)),
            pltpu.SemaphoreType.DMA((recvs,)),
            pltpu.SemaphoreType.DMA((locals_,)),
        ],
        compiler_params=pltpu.CompilerParams(
            collective_id=collective_id, has_side_effects=True, vmem_limit_bytes=VMEM_LIMIT
        ),
    )(*args)


def gather_kernel(xs, wj, sg, gains, xg, wg, sgg, gg, send, recv, loc):
    x, y, z, c = place()
    low, high = y % 2, y // 2
    me = device(x, y, z, c)
    group = x * 2 + c
    chunk = x * 2 + low
    a = x * (1 - c) + y * c
    b = y * (1 - c) + x * c

    def at(first, second):
        return first * (1 - c) + second * c, second * (1 - c) + first * c

    def dev_at(first, second):
        px, py = at(first % 4, second % 4)
        return device(px, py, z, c)

    def slot_at(first, second):
        px, py = at(first % 4, second % 4)
        return row_slot(px, py, c)

    a_up, a_down = dev_at(a + 1, b), dev_at(a + 3, b)
    b_up, b_down = dev_at(a, b + 1), dev_at(a, b + 3)
    z_up, z_down = device(x, y, (z + 1) % NZ, c), device(x, y, (z + 7) % NZ, c)
    twin = device(x, y, z, 1 - c)
    targets = []
    for d in range(GROUP):
        there = (group + d) % GROUP
        targets.append((device(there // 2, high * 2 + c, z, there % 2), there))
    origins = [device(k // 2, high * 2 + k % 2, z, low) for k in range(GROUP)]
    stays = low == c

    barrier = pltpu.get_barrier_semaphore()
    for near in (a_up, a_down, b_up, b_down, z_up, z_down, twin):
        pl.semaphore_signal(barrier, inc=1, device_id=near, device_id_type=MESH)
    for k, origin in enumerate(origins):

        @pl.when(jnp.logical_not(stays & (chunk == k)))
        def _():
            pl.semaphore_signal(barrier, inc=1, device_id=origin, device_id_type=MESH)

    @pl.when(stays)
    def _():
        pl.semaphore_wait(barrier, 7 + GROUP - 1)

    @pl.when(jnp.logical_not(stays))
    def _():
        pl.semaphore_wait(barrier, 7 + GROUP)

    mover = Mover(send, recv, me)
    own = slot_at(a, b)
    A1, A2, B1U, B1D, B2U, B2D, TWIN, ZW, GAIN, SIGN = 8, 10, 12, 16, 20, 24, 28, 44, 52, 53
    KEPT = 59

    def kept(part, remote):
        source = wj.at[group] if part == 0 else sg.at[group]
        landed = wg.at[:, x, z, low] if part == 0 else sgg.at[chunk]
        if not remote:
            return pltpu.make_async_copy(source, landed, loc.at[part])
        return pltpu.make_async_remote_copy(
            src_ref=source,
            dst_ref=landed,
            send_sem=send.at[KEPT + part],
            recv_sem=recv.at[chunk + SIGN * part],
            device_id=targets[0][0],
            device_id_type=MESH,
        )

    def start_kept(part):
        @pl.when(stays)
        def _():
            kept(part, False).start()

        @pl.when(jnp.logical_not(stays))
        def _():
            kept(part, True).start()

    def arrive_all(part, ref):
        for k in range(GROUP):
            mine = stays & (chunk == k)

            @pl.when(mine)
            def _():
                kept(part, False).wait()

            @pl.when(jnp.logical_not(mine))
            def _():
                mover.got(ref, k + SIGN * part)

    start_kept(0)
    for peer, there in targets[1:]:
        mover.put(wj.at[there], wg.at[:, x, z, low], chunk, peer)
    mover.put(xs, xg.at[:, own], A1, a_up)
    mover.put(xs, xg.at[:, own], A1 + 1, a_down)
    mover.put(xs, xg.at[:, own], B1U, b_up)
    mover.put(xs, xg.at[:, own], B1D, b_down)
    mover.put(xs, xg.at[:, own], TWIN, twin)
    mover.put(gains, gg.at[c], GAIN, twin)
    own_rows = pltpu.make_async_copy(xs, xg.at[:, own], loc.at[2])
    own_gains = pltpu.make_async_copy(gains, gg.at[c], loc.at[3])
    own_rows.start()
    own_gains.start()
    start_kept(1)
    for peer, there in targets[1:]:
        mover.put(sg.at[there], sgg.at[chunk], SIGN + chunk, peer)

    arrive_all(0, wg.at[:, x, z, low])

    def z_step(t, source_down, source_up):
        if t < 4:
            mover.put(wg.at[:, :, source_down], wg.at[:, :, source_down], ZW + 2 * (t - 1), z_up)
            mover.put(wg.at[:, :, source_up], wg.at[:, :, source_up], ZW + 2 * (t - 1) + 1, z_down)
        else:
            mover.put(wg.at[0, :, source_down], wg.at[0, :, source_down], ZW + 6, z_up)
            mover.put(wg.at[1, :, source_up], wg.at[1, :, source_up], ZW + 7, z_down)

    def z_got(t):
        down, up = (z + 8 - t) % NZ, (z + t) % NZ
        mover.got(wg.at[:, :, down], ZW + 2 * (t - 1))
        mover.got(wg.at[:, :, up], ZW + 2 * (t - 1) + 1)
        return down, up

    z_step(1, z, z)

    def spread(slot, k):
        shard = xg.at[:, slot]
        mover.put(shard, shard, B1U + k, b_up)
        mover.put(shard, shard, B1D + k, b_down)
        mover.put(shard, shard, TWIN + k, twin)

    from_down, from_up, far = slot_at(a + 3, b), slot_at(a + 1, b), slot_at(a + 2, b)
    mover.got(xg.at[:, from_down], A1)
    mover.put(xg.at[0, from_down], xg.at[0, from_down], A2, a_up)
    spread(from_down, 1)
    mover.got(xg.at[:, from_up], A1 + 1)
    mover.put(xg.at[1, from_up], xg.at[1, from_up], A2 + 1, a_down)
    spread(from_up, 2)
    mover.got(xg.at[0, far], A2)
    mover.got(xg.at[1, far], A2 + 1)
    spread(far, 3)

    def second(k, first):
        down, up = slot_at(first, b + 3), slot_at(first, b + 1)
        mover.got(xg.at[:, down], B1U + k)
        mover.put(xg.at[0, down], xg.at[0, down], B2U + k, b_up)
        mover.put(xg.at[:, down], xg.at[:, down], TWIN + 4 + k, twin)
        mover.got(xg.at[:, up], B1D + k)
        mover.put(xg.at[1, up], xg.at[1, up], B2D + k, b_down)
        mover.put(xg.at[:, up], xg.at[:, up], TWIN + 8 + k, twin)

    def second_far(k, first):
        opposite = slot_at(first, b + 2)
        mover.got(xg.at[0, opposite], B2U + k)
        mover.got(xg.at[1, opposite], B2D + k)
        mover.put(xg.at[:, opposite], xg.at[:, opposite], TWIN + 12 + k, twin)

    second(0, a)
    down, up = z_got(1)
    z_step(2, down, up)
    second(1, a + 3)
    second(2, a + 1)
    down, up = z_got(2)
    z_step(3, down, up)
    second(3, a + 2)
    second_far(0, a)
    second_far(1, a + 3)
    down, up = z_got(3)
    z_step(4, down, up)
    second_far(2, a + 1)
    second_far(3, a + 2)
    opposite = (z + 4) % NZ
    arrive_all(1, sgg.at[chunk])
    for k in range(16):
        mover.got(xg.at[:, own], TWIN + k)
    mover.got(gg.at[c], GAIN)
    mover.got(wg.at[0, :, opposite], ZW + 6)
    mover.got(wg.at[1, :, opposite], ZW + 7)
    own_rows.wait()
    own_gains.wait()
    assert len(mover.sent) == KEPT, len(mover.sent)
    mover.finish()

    @pl.when(jnp.logical_not(stays))
    def _():
        for part in range(2):
            kept(part, True).wait_send()


def project_kernel(x_ref, w_ref, s_ref, gain_ref, keep_ref, y_ref):
    mean_part = jnp.dot(x_ref[0], w_ref[0], preferred_element_type=F32)
    delta_part = jnp.dot(x_ref[1], w_ref[1], preferred_element_type=F32)
    both = (mean_part + s_ref[...].astype(F32) * delta_part).astype(BF16).astype(F32)
    for e in range(2):
        unit = both[:, e * HEAD : (e + 1) * HEAD]
        inverse = lax.rsqrt(jnp.mean(unit * unit, axis=-1, keepdims=True) + EPSILON)
        normed = unit * inverse * gain_ref[e : e + 1, :]
        y_ref[e] = jnp.where(keep_ref[e : e + 1, :] > 0, unit, normed).astype(BF16)


def attention_kernel(
    heads, factor, y_ref, mix, wo, att, mixg, wog,
    kv, q, wos, acc, up_out, down_out, up_in, down_in, att_own, send, recv, loc,
):
    x, y, z, c = place()
    low, high = y % 2, y // 2
    me = device(x, y, z, c)
    own = x * 2 + c
    rows = q.shape[2]
    units = 3 * heads
    half = att_own.shape[1] // HEAD + 1
    half = half // 2 * HEAD
    peers = [group_peer(x, y, z, c, d) for d in range(1, GROUP)]
    aligned = [device((x + d) % NX, y, z, c) for d in range(1, NX)]
    twin = device(x, y, z, 1 - c)
    swap = device(x, high * 2 + c, z, low)
    z_up, z_down = device(x, y, (z + 1) % NZ, c), device(x, y, (z + 7) % NZ, c)
    moves = low != c
    stays = low == c

    barrier = pltpu.get_barrier_semaphore()
    for near in [peer for peer, _ in peers] + [z_up, z_down]:
        pl.semaphore_signal(barrier, inc=1, device_id=near, device_id_type=MESH)

    @pl.when(moves)
    def _():
        pl.semaphore_signal(barrier, inc=1, device_id=swap, device_id_type=MESH)
        pl.semaphore_wait(barrier, GROUP + 2)

    @pl.when(stays)
    def _():
        pl.semaphore_wait(barrier, GROUP + 1)

    Q, R_SWAP, SIGNS, ATT, WO, SUMS = units, units + 14, units + 16, units + 23, units + 30, units + 38
    FORWARD, SWAP = 14, 14 + 2 * heads
    mover = Mover(send, recv, me, SWAP + 2)

    def copy_to(src, dst, s, r, where):
        return pltpu.make_async_remote_copy(
            src_ref=src,
            dst_ref=dst,
            send_sem=send.at[s],
            recv_sem=recv.at[r],
            device_id=where,
            device_id_type=MESH,
        )

    def own_copies(n):
        e = n % 2
        if n < heads:
            return [
                copy_to(y_ref.at[e, pl.ds(there * rows, rows)], q.at[z, n], e * 7 + d, n, peer)
                for d, (peer, there) in enumerate(peers)
            ]
        landed = kv.at[n - heads]
        return [
            copy_to(y_ref.at[e], landed, e * 7 + d, n, peer)
            for d, peer in enumerate(aligned + [twin])
        ]

    def kept(n):
        source = y_ref.at[n % 2]
        if n < heads:
            return pltpu.make_async_copy(source.at[pl.ds(own * rows, rows)], q.at[z, n], loc.at[n % 2])
        return pltpu.make_async_copy(source, kv.at[n - heads], loc.at[n % 2])

    for n in range(units):

        @pl.when(own == n // 2)
        def _():
            for copy in own_copies(n):
                copy.start()
            kept(n).start()

    def swapped(part, remote):
        source = mix if part == 0 else wo
        landed = mixg.at[x * 2 + low] if part == 0 else wos
        if remote:
            return copy_to(source, landed, SWAP + part, R_SWAP + part, swap)
        return pltpu.make_async_copy(source, landed, loc.at[2 + part])

    @pl.when(moves)
    def _():
        for part in range(2):
            swapped(part, True).start()

    @pl.when(stays)
    def _():
        for part in range(2):
            swapped(part, False).start()

    def arrive(n):
        landed = q.at[z, n] if n < heads else kv.at[n - heads]

        @pl.when(own == n // 2)
        def _():
            kept(n).wait()

        @pl.when(own != n // 2)
        def _():
            copy_to(landed, landed, 0, n, me).wait_recv()

    def forward(n):
        landed = kv.at[n - heads]
        return copy_to(landed, landed, FORWARD + n - heads, n, twin)

    def forwards(n):
        return (own != n // 2) & (c == (n // 2) % 2)

    for n in range(heads):
        arrive(n)

    cut = (heads + 1) // 2
    pieces = [pl.ds(0, cut), pl.ds(cut, heads - cut)]

    def q_slot(t, way, piece):
        return Q + (4 * (t - 1) + 2 * way + piece if t < 4 else 12 + way)

    def ring_step(t):
        for piece in range(2):
            for way in range(2):
                plane = (z + 8 - (t - 1)) % NZ if way == 0 else (z + t - 1) % NZ
                block = q.at[plane, pieces[piece]]
                if t > 1:
                    mover.got(block, q_slot(t - 1, way, piece))
                if t < 4 or piece == way:
                    mover.put(block, block, q_slot(t, way, piece), z_down if way else z_up)

    def wo_step(t):
        for way in range(2):
            plane = (z + 8 - (t - 1)) % NZ if way == 0 else (z + t - 1) % NZ
            if t == 1:
                block = wos
            else:
                block = wog.at[:, plane]
                mover.got(block, WO + 2 * (t - 2) + way)
            where = z_down if way else z_up
            if t < 4:
                mover.put(block, wog.at[:, plane], WO + 2 * (t - 1) + way, where)
            else:
                mover.put(wog.at[way, plane], wog.at[way, plane], WO + 6 + way, where)

    ring_step(1)

    @pl.when(moves)
    def _():
        mover.got(wos, R_SWAP + 1)
        mover.got(mixg.at[own], R_SWAP)

    @pl.when(stays)
    def _():
        for part in range(2):
            swapped(part, False).wait()

    wo_step(1)
    wo_own = pltpu.make_async_copy(wos, wog.at[:, z], loc.at[2])
    wo_own.start()
    for t in range(2, 5):
        for n in range(heads, units):
            if (n - heads) % 3 == t - 2:

                @pl.when(own == n // 2)
                def _():
                    kept(n).wait()

                @pl.when(forwards(n))
                def _():
                    landed = kv.at[n - heads]
                    copy_to(landed, landed, 0, n, me).wait_recv()
                    forward(n).start()

        ring_step(t)
    wo_step(2)
    for n in range(heads, units):

        @pl.when(c != (n // 2) % 2)
        def _():
            landed = kv.at[n - heads]
            copy_to(landed, landed, 0, n, me).wait_recv()

    far = (z + 4) % NZ
    for way in range(2):
        mover.got(q.at[far, pieces[way]], q_slot(4, way, way))

    def group_send(source, out, slot):
        for d, peer in enumerate(aligned):
            mover.put(source, out.at[own], slot + d, peer)
        mover.put(source, out.at[own], slot + 3, twin)

    def group_pass(out, slot):
        for d in (0, 2, 1):
            there = ((x + NX - 1 - d) % NX) * 2 + c
            mover.got(out.at[there], slot + d)
            mover.put(out.at[there], out.at[there], slot + 4 + d, twin)

    def group_end(out, slot):
        for k in range(NX):
            mover.got(out.at[own], slot + 3 + k)

    group_send(mixg.at[own], mixg, SIGNS)

    lane = lax.broadcasted_iota(jnp.int32, (rows, HEAD), 1)
    tail = heads * HEAD

    def plane_sums(planes):
        for p in planes:
            acc[p, :, tail:] = jnp.zeros((rows, HEAD), F32)

        def one(head, unused):
            block = [q[p, head] for p in planes]
            block = block[0] if len(block) == 1 else jnp.concatenate(block, axis=0)
            scores = lax.dot_general(
                block, kv[head], (((1,), (1,)), ((), ())), preferred_element_type=F32
            )
            weights = jnp.exp2(scores * factor).astype(BF16)
            values = kv[heads + head]
            values = jnp.concatenate([values, jnp.ones_like(values)], axis=1)
            sums = jnp.dot(weights, values, preferred_element_type=F32)
            columns = pl.ds(pl.multiple_of(head * HEAD, HEAD), HEAD)
            for k, p in enumerate(planes):
                piece = sums[k * rows : (k + 1) * rows]
                acc[p, :, columns] = piece[:, :HEAD]
                acc[p, :, tail:] = jnp.where(lane == head, piece[:, HEAD:], acc[p, :, tail:])
            return unused

        lax.fori_loop(0, heads, one, 0)

    sides = [pl.ds(0, half), pl.ds(half, half)]

    def s_slot(t, way, side):
        return SUMS + (way if t == 0 else 2 + 4 * (t - 1) + 2 * way + side)

    outs, ins = [up_out, down_out], [up_in, down_in]
    plane_sums([far])
    for way in range(2):
        outs[way][0, :, sides[way]] = acc[far, :, sides[way]].astype(BF16)
        mover.put(
            outs[way].at[0, :, sides[way]],
            ins[way].at[0, :, sides[way]],
            s_slot(0, way, way),
            z_down if way else z_up,
        )
    for t in range(1, 4):
        goals = [(z + 4 - t) % NZ, (z + 4 + t) % NZ]
        plane_sums(goals)
        for side in range(2):
            for way in range(2):
                value = acc[goals[way], :, sides[side]]
                if t > 1 or side == way:
                    mover.got(ins[way].at[t - 1, :, sides[side]], s_slot(t - 1, way, side))
                    value = value + ins[way][t - 1, :, sides[side]].astype(F32)
                outs[way][t, :, sides[side]] = value.astype(BF16)
                mover.put(
                    outs[way].at[t, :, sides[side]],
                    ins[way].at[t, :, sides[side]],
                    s_slot(t, way, side),
                    z_down if way else z_up,
                )
        if t == 1:
            group_pass(mixg, SIGNS)
    plane_sums([z])
    wo_step(3)
    for side in (1, 0):
        for way in range(2):
            mover.got(ins[way].at[3, :, sides[side]], s_slot(3, way, side))
    totals = acc[z, :, tail:]
    for way in range(2):
        totals = totals + ins[way][3, :, tail:].astype(F32)
    for h in range(heads):
        columns = slice(h * HEAD, (h + 1) * HEAD)
        value = acc[z, :, columns]
        for way in range(2):
            value = value + ins[way][3, :, columns].astype(F32)
        att_own[:, columns] = (value / totals[:, h : h + 1]).astype(BF16)
    att_kept = pltpu.make_async_copy(att_own, att.at[own], loc.at[3])
    att_kept.start()
    group_send(att_own, att, ATT)
    wo_step(4)
    group_pass(att, ATT)
    group_end(mixg, SIGNS)
    for way in range(2):
        mover.got(wog.at[way, far], WO + 6 + way)
    group_end(att, ATT)
    wo_own.wait()
    att_kept.wait()
    mover.finish()
    for n in range(units):

        @pl.when(own == n // 2)
        def _():
            for copy in own_copies(n):
                copy.wait_send()

        if n >= heads:

            @pl.when(forwards(n))
            def _():
                forward(n).wait_send()

    @pl.when(moves)
    def _():
        for part in range(2):
            swapped(part, True).wait_send()


def out_kernel(a_ref, s_ref, w_ref, o_ref):
    plain = a_ref[...]
    flipped = (plain.astype(F32) * s_ref[...].astype(F32)).astype(BF16)
    for m, rows in enumerate((plain, flipped)):
        o_ref[m] = lax.dot_general(
            rows, w_ref[m], (((1,), (1,)), ((), ())), preferred_element_type=F32
        ).astype(BF16)


def owner_scatter_kernel(part, out, send, recv, loc):
    x, y, z, c = place()
    own = row_slot(x, y, c)
    landing = (x * 2 + c) * NY + y
    count = NX * NY * NC
    peers = []
    for d in range(1, count):
        there = (own + d) % count
        peers.append(
            (device(there // 8, ((there // 2) % 2) * 2 + (there // 4) % 2, z, there % 2), there)
        )
    greet([peer for peer, _ in peers], len(peers))
    mover = Mover(send, recv, device(x, y, z, c))
    local = pltpu.make_async_copy(part.at[:, own], out.at[:, landing], loc.at[0])
    local.start()
    for d, (peer, there) in enumerate(peers, 1):
        mover.put(part.at[:, there], out.at[:, landing], d - 1, peer)
    for d in range(1, count):
        mover.got(out.at[:, landing], d - 1)
    local.wait()
    mover.finish()


def vmem(count):
    return [pl.BlockSpec(memory_space=pltpu.VMEM)] * count


def body(
    tokens, in_bits, qkv_weights, qkv_bits, gain_query, gain_key, out_weights, mix_bits, out_bits
):
    own_rows, width = tokens.shape
    depth, columns = qkv_weights.shape[2], qkv_weights.shape[3]
    heads = columns // HEAD
    rows = qkv_bits.shape[0]
    plane_rows = rows * GROUP
    x, y, _, c = place()
    group = x * 2 + c

    flipped = (tokens.astype(F32) * signed(in_bits)).astype(BF16)
    shard = jnp.stack([tokens, flipped])
    units = jnp.transpose(qkv_weights.reshape(2, 3, depth, heads, HEAD), (1, 3, 0, 2, 4))
    units = units.reshape(3 * heads, 2, depth, HEAD)
    units = jnp.concatenate([units, units[-1:]])
    wj = jnp.transpose(units.reshape(GROUP, 2, 2, depth, HEAD), (0, 2, 3, 1, 4))
    wj = wj.reshape(GROUP, 2, depth, 2 * HEAD)
    wo = jnp.transpose(out_weights, (0, 2, 1))
    signs = signed(qkv_bits).astype(BF16).reshape(rows, 3 * heads * HEAD)
    signs = jnp.concatenate([signs, signs[:, -HEAD:]], axis=1)
    signs = jnp.transpose(signs.reshape(rows, GROUP, 2 * HEAD), (1, 0, 2))

    gains = jnp.stack([gain_query.reshape(heads, HEAD), gain_key.reshape(heads, HEAD)])

    xg, wg, sgg, gg = comm(
        gather_kernel,
        (shard, wj, signs, gains),
        [
            jax.ShapeDtypeStruct((2, NX * NY * NC, own_rows, width), BF16),
            jax.ShapeDtypeStruct((2, NX, NZ, 2, depth, 2 * HEAD), BF16),
            jax.ShapeDtypeStruct((GROUP, rows, 2 * HEAD), BF16),
            jax.ShapeDtypeStruct((2,) + gains.shape, F32),
        ],
        61,
        61,
        4,
        0,
    )

    gains = lax.dynamic_index_in_dim(gg, y % 2, 0, keepdims=False).reshape(2 * heads, HEAD)
    gains = jnp.concatenate([gains, jnp.ones((heads + 1, HEAD), F32)])
    gain = lax.dynamic_slice_in_dim(gains, group * 2, 2, 0)
    keep = (group * 2 + jnp.arange(2) >= 2 * heads).astype(F32)[:, None] * jnp.ones((1, HEAD), F32)

    step = 128
    units = pl.pallas_call(
        project_kernel,
        grid=(plane_rows // step,),
        out_shape=jax.ShapeDtypeStruct((2, plane_rows, HEAD), BF16),
        in_specs=[
            pl.BlockSpec((2, step, width), lambda i: (0, i, 0)),
            pl.BlockSpec((2, width, 2 * HEAD), lambda i: (0, 0, 0)),
            pl.BlockSpec((step, 2 * HEAD), lambda i: (i, 0)),
            pl.BlockSpec((2, HEAD), lambda i: (0, 0)),
            pl.BlockSpec((2, HEAD), lambda i: (0, 0)),
        ],
        out_specs=pl.BlockSpec((2, step, HEAD), lambda i: (0, i, 0)),
        compiler_params=pltpu.CompilerParams(vmem_limit_bytes=VMEM_LIMIT),
    )(
        xg.reshape(2, plane_rows, width),
        wg.reshape(2, width, 2 * HEAD),
        sgg.reshape(plane_rows, 2 * HEAD),
        gain,
        keep,
    )

    mix = signed(mix_bits).astype(BF16)
    packed = (heads + 1) * HEAD
    att, mixg, wog = comm(
        functools.partial(attention_kernel, heads, math.log2(math.e) / math.sqrt(HEAD)),
        (units, mix, wo),
        [
            jax.ShapeDtypeStruct((GROUP, rows, columns), BF16),
            jax.ShapeDtypeStruct((GROUP, rows, columns), BF16),
            jax.ShapeDtypeStruct((2, NZ) + wo.shape[1:], BF16),
        ],
        66 + 2 * heads,
        3 * heads + 52,
        4,
        1,
        [
            pltpu.VMEM((2 * heads, plane_rows, HEAD), BF16),
            pltpu.VMEM((NZ, heads, rows, HEAD), BF16),
            pltpu.VMEM(wo.shape, BF16),
            pltpu.VMEM((NZ, rows, packed), F32),
        ]
        + [pltpu.VMEM((4, rows, packed), BF16)] * 4
        + [pltpu.VMEM((rows, columns), BF16)],
    )
    out_columns = NZ * wo.shape[1]
    partial_out = pl.pallas_call(
        out_kernel,
        out_shape=jax.ShapeDtypeStruct((2, plane_rows, out_columns), BF16),
        in_specs=vmem(3),
        out_specs=pl.BlockSpec(memory_space=pltpu.VMEM),
        compiler_params=pltpu.CompilerParams(vmem_limit_bytes=VMEM_LIMIT),
    )(
        att.reshape(plane_rows, columns),
        mixg.reshape(plane_rows, columns),
        wog.reshape(2, out_columns, columns),
    )

    count = NX * NY * NC
    (landed,) = comm(
        owner_scatter_kernel,
        (partial_out.reshape(2, count, own_rows, out_columns),),
        [jax.ShapeDtypeStruct((2, count, own_rows, out_columns), BF16)],
        count - 1,
        count - 1,
        1,
        4,
    )
    summed = jnp.sum(landed.astype(F32).reshape(2, GROUP, 4, own_rows, out_columns), axis=2)
    summed = summed.reshape(2, NX, 2, own_rows, NZ, out_columns // NZ)
    summed = jnp.transpose(summed, (0, 3, 1, 4, 2, 5)).reshape(2, own_rows, width)
    own_bits = lax.dynamic_slice_in_dim(out_bits, lax.axis_index("uly") * own_rows, own_rows, 0)
    return (summed[0] + signed(own_bits) * summed[1]).astype(BF16)


def solution(mesh):
    return jax.shard_map(
        body,
        mesh=mesh,
        in_specs=(
            P(("blk", "uly"), None),
            P(("blk", "uly"), None),
            P(None, None, "blk", "uly"),
            P("blk", None, "uly"),
            P("uly"),
            P("uly"),
            P(None, "uly", "blk"),
            P("blk", "uly"),
            P("blk", None),
        ),
        out_specs=P(("blk", "uly"), None),
        check_vma=False,
    )
```
